32 devices in a mesh: dp: 8 (over y, x, core), seq: 4 (over z).
Axes of the slice: x: 2, y: 2, z: 4, core: 2. Of those that a mesh axis runs over, the one named last changes fastest.
Arguments:
- tokens: bfloat16 [8, 1024, 1280], P('dp', 'seq'), may hold values from -6 to 6
- tube_index: int32 [8, 1024], P('dp', 'seq'), may hold values from 0 to 16383
- counts: int32 [8, 4], P('dp', 'seq'), may hold values from 128 to 256
- qkv_weight: bfloat16 [1280, 3840], P('dp'), may hold values from -4 to 4
- proj_weight: bfloat16 [1280, 1280], P('dp'), may hold values from -0.15625 to 0.15625
- ctx_b: bfloat16 [8, 1024, 1280], P('dp', 'seq'), may hold values from -12 to 12
- cot_b: bfloat16 [8, 1024, 1280], P('dp', 'seq'), may hold values from -12 to 12
- b_counts: int32 [8, 4], P('dp', 'seq'), may hold values from 128 to 256
Outputs:
- out_a: bfloat16 [8, 1024, 1280], P('dp', 'seq')
- weight_grad: float32 [1280, 1280], P('dp')
The draws below stay inside these ranges and needn't reach their ends.
Inputs may be any that keep to these rules, and one draw needn't show every extreme that they name: `counts`: slots of a device's block past its count hold padding. `b_counts`: slots of a device's block past its count hold padding.
All inputs are finite; a program needn't handle non-finite values.
Results may differ from the reference program's by a relative error of at most 0.017.
Values may be sent and summed in bfloat16 or wider, within the bound.
A program may use at most 128 MiB of HBM per device.

```python
import math
import jax
import jax.numpy as jnp
from jax import lax

D = 1280
HEADS = 16
CAP = 256
TUBES = 16384
CLIPS = 8
SLOTS = 1024
N_SEQ = 4


def draw_qkv_weight(key, part):
    base_key = jax.random.fold_in(jax.random.fold_in(key, 11), 0)
    weight = jax.random.normal(base_key, (D, 3 * D), jnp.float32) / jnp.sqrt(jnp.float32(D))
    return jnp.clip(weight, -4.0, 4.0).astype(jnp.bfloat16)


def draw_ctx_b(key, part):
    noise_key = jax.random.fold_in(jax.random.fold_in(key, 23), 0)
    values = jax.random.normal(noise_key, (CLIPS, SLOTS, D), jnp.float32)
    return jnp.clip(values, -12.0, 12.0).astype(jnp.bfloat16)


def draw_cot_b(key, part):
    noise_key = jax.random.fold_in(jax.random.fold_in(key, 37), 0)
    values = jax.random.normal(noise_key, (CLIPS, SLOTS, D), jnp.float32)
    return jnp.clip(values, -12.0, 12.0).astype(jnp.bfloat16)


def set_ends(drawn, key, smallest, top_value):
    longest = drawn.shape.index(max(drawn.shape))
    spots = []
    for shift in (0, 1):
        where = [jax.random.randint(jax.random.fold_in(key, axis), (), 0, length) for axis, length in enumerate(drawn.shape)]
        where[longest] = (where[longest] + shift) % drawn.shape[longest]
        spots.append(tuple(where))
    return drawn.at[spots[0]].set(smallest).at[spots[1]].set(top_value)


def steps_of(key, extent, shards, low, high):
    def one(dim, blocks):
        steps = jax.random.uniform(jax.random.fold_in(jax.random.fold_in(key, 6), dim), (blocks,), jnp.float32, low / len(shards), high / len(shards))
        return jnp.repeat(jnp.exp(steps), extent[dim] // blocks).reshape((-1,) + (1,) * (len(extent) - dim - 1))

    gain = one(*shards[0])
    for cut in shards[1:]:
        gain = gain * one(*cut)
    return gain


def normal_values(stream_key, dims, scale, limit, pieces=(), kind=jnp.bfloat16):
    entries = scale * jax.random.normal(stream_key, dims, jnp.float32)
    if pieces:
        entries = entries * steps_of(stream_key, dims, pieces, -0.22, 0.18)
    return jnp.clip(entries, -limit, limit).astype(kind)


def setup_inputs(seed: int = 0) -> dict:
    keys = jax.random.split(jax.random.key(seed), 9)
    tokens = normal_values(keys[0], (CLIPS, SLOTS, D), 1.0, 6.0, ((0, 8), (1, 4)))
    tube_index = set_ends(jax.random.randint(keys[1], (CLIPS, SLOTS), 0, TUBES), jax.random.fold_in(keys[1], 1), 0, TUBES - 1).astype(jnp.int32)
    counts = set_ends(jax.random.randint(keys[2], (CLIPS, N_SEQ), CAP // 2, CAP + 1), jax.random.fold_in(keys[2], 1), CAP // 2, CAP).astype(jnp.int32)
    qkv_weight = draw_qkv_weight(jax.random.fold_in(keys[8], 71), 0)
    proj_weight = normal_values(keys[4], (D, D), D ** -0.5, 0.15625, ((0, 8),))
    ctx_b = draw_ctx_b(jax.random.fold_in(keys[8], 71), 0)
    cot_b = draw_cot_b(jax.random.fold_in(keys[8], 71), 0)
    b_counts = set_ends(jax.random.randint(keys[7], (CLIPS, N_SEQ), CAP // 2, CAP + 1), jax.random.fold_in(keys[7], 1), CAP // 2, CAP).astype(jnp.int32)
    return dict(tokens=tokens, tube_index=tube_index, counts=counts, qkv_weight=qkv_weight, proj_weight=proj_weight, ctx_b=ctx_b, cot_b=cot_b, b_counts=b_counts)


def embed(tube_ids, model_width):
    half_width = model_width // 2
    positions = jnp.arange(half_width, dtype=jnp.float32)
    frequency = jnp.exp(positions * (-2.0 * math.log(10000.0) / model_width))
    angles = tube_ids.astype(jnp.float32)[:, None] * frequency[None, :]
    return jnp.concatenate([jnp.sin(angles), jnp.cos(angles)], axis=1)

def layer_norm(values):
    centered = values - lax.optimization_barrier(jnp.mean(values, axis=1, keepdims=True))
    spread = lax.optimization_barrier(jnp.mean(centered * centered, axis=1, keepdims=True))
    return centered * lax.rsqrt(spread + 1e-06)

def attend_head(head_in):
    query_rows, key_rows, value_rows, valid_keys = head_in
    seq_length = key_rows.shape[0]
    block_rows = math.gcd(seq_length, 512)
    head_width = query_rows.shape[1]
    score_scale = 1.0 / math.sqrt(head_width)
    blocked = query_rows.reshape(seq_length // block_rows, block_rows, head_width)

    def one_block(block_query):
        scores = jnp.dot(block_query, key_rows.T, preferred_element_type=jnp.float32) * score_scale
        scores = jnp.where(valid_keys[None, :], scores, -1e+30)
        top_score = lax.optimization_barrier(jnp.max(scores, axis=1, keepdims=True))
        exponent = jnp.exp(scores - top_score)
        weights = (exponent / lax.optimization_barrier(jnp.sum(exponent, axis=1, keepdims=True))).astype(jnp.bfloat16)
        return jnp.dot(weights, value_rows, preferred_element_type=jnp.float32).astype(jnp.bfloat16)
    return lax.map(one_block, blocked).reshape(seq_length, head_width)

def clip_layer(clip_in, qkv_weight, proj_weight):
    clip_tokens, clip_index, clip_counts = clip_in
    with_pos = clip_tokens.astype(jnp.float32) + embed(clip_index, D)
    normed = layer_norm(with_pos).astype(jnp.bfloat16)
    projected = jnp.dot(normed, qkv_weight, preferred_element_type=jnp.float32).astype(jnp.bfloat16)
    slot_ids = jnp.arange(CAP, dtype=jnp.int32)
    valid = (slot_ids[None, :] < clip_counts[:, None]).reshape(SLOTS)
    head_width = D // HEADS
    split_heads = projected.reshape(SLOTS, 3, HEADS, head_width).transpose(1, 2, 0, 3)
    valid_heads = jnp.broadcast_to(valid[None, :], (HEADS, SLOTS))
    context = lax.map(attend_head, (split_heads[0], split_heads[1], split_heads[2], valid_heads))
    context = context.transpose(1, 0, 2).reshape(SLOTS, D)
    output = with_pos + jnp.dot(context, proj_weight, preferred_element_type=jnp.float32)
    return output.astype(jnp.bfloat16)

def reference(tokens, tube_index, counts, qkv_weight, proj_weight, ctx_b, cot_b, b_counts):

    def per_clip(clip_in):
        return clip_layer(clip_in, qkv_weight, proj_weight)
    out_a = lax.map(per_clip, (tokens, tube_index, counts))
    slot_ids = jnp.arange(CAP, dtype=jnp.int32)
    b_valid = (slot_ids[None, None, :] < b_counts[:, :, None]).reshape(CLIPS * SLOTS, 1)
    masked_cot = jnp.where(b_valid, cot_b.reshape(CLIPS * SLOTS, D), jnp.zeros((), jnp.bfloat16))
    summed = lax.dot_general(ctx_b.reshape(CLIPS * SLOTS, D), masked_cot, (((0,), (0,)), ((), ())), preferred_element_type=jnp.float32)
    weight_grad = summed / math.sqrt(CLIPS * SLOTS)
    return (out_a, weight_grad)
```

```python
import functools
import math

import jax
import jax.numpy as jnp
from jax import lax
from jax.experimental import pallas as pl
from jax.experimental.pallas import tpu as pltpu
from jax.sharding import PartitionSpec as P

HEADS = 16


def layer_norm(values):
    centered = values - jnp.mean(values, axis=1, keepdims=True)
    spread = jnp.mean(centered * centered, axis=1, keepdims=True)
    return centered * lax.rsqrt(spread + 1e-06)


LANES = 128
MESH = pl.DeviceIdType.MESH
LOG2_E = math.log2(math.e)


def round_up(value, unit):
    return (value + unit - 1) // unit * unit


def window(width, seq_count, head_cols):
    size = max(owner * head_cols % LANES + head_cols for owner in range(seq_count))
    size = round_up(size, LANES)
    return size, [min(owner * head_cols // LANES * LANES, width - size) for owner in range(seq_count)]


def block_kernel(
    dp_count, seq_count, heads_here, head_width,
    tok_ref, index_ref, freq_ref, count_ref, bcount_ref, w_ref, proj_ref, ctxb_ref, cot_ref,
    out_ref, grad_ref,
    x_all, bias_all, w_all, p_all, qkv, acc, ctx_send, ctx_all,
    g_part, g_sib, g_chip, g_recv, g_seq, pos, index_col, ctxb, cot,
    l_sems, xr_sems, xl_sems, bias_sems, w_sems, w_fsems, p_sems, p_fsems, c_sems, gs_sems, gr_sems,
    ar_sems, al_sems,
):
    d = lax.axis_index("dp")
    s = lax.axis_index("seq")
    core = lax.rem(d, 2)
    chip = lax.div(d, 2)
    chips = dp_count // 2
    sibling = chip * 2 + 1 - core
    slots, width = tok_ref.shape
    rows = w_ref.shape[0]
    head_cols = heads_here * head_width
    part, starts = window(width, seq_count, head_cols)
    offsets = [owner * head_cols - start for owner, start in enumerate(starts)]
    first_lane = lax.min(lax.div(s * head_cols, LANES) * LANES, width - part)
    offset = s * head_cols - first_lane

    def ahead(v):
        return lax.rem(chip + v, chips)

    def behind(v):
        return lax.rem(chip + chips - v, chips)

    def seq_ahead(k):
        return lax.rem(s + k, seq_count)

    def seq_behind(k):
        return lax.rem(s + seq_count - k, seq_count)

    def row_block(index):
        return pl.ds(pl.multiple_of(index * rows, rows), rows)

    def slot_block(index):
        return pl.ds(pl.multiple_of(index * slots, slots), slots)

    def to_dp(src, dst, sems, index, target):
        return pltpu.make_async_remote_copy(
            src_ref=src, dst_ref=dst, send_sem=sems.at[0, index], recv_sem=sems.at[1, index],
            device_id={"dp": target, "seq": s}, device_id_type=MESH,
        )

    def to_seq(src, dst, sems, index, target):
        return pltpu.make_async_remote_copy(
            src_ref=src, dst_ref=dst, send_sem=sems.at[0, index], recv_sem=sems.at[1, index],
            device_id={"dp": d, "seq": target}, device_id_type=MESH,
        )

    local = [
        pltpu.make_async_copy(
            w_ref.at[:, pl.ds(pl.multiple_of(kind * width + first_lane, LANES), part)],
            w_all.at[row_block(d), kind * part:(kind + 1) * part], l_sems.at[kind],
        )
        for kind in range(3)
    ]
    local.append(pltpu.make_async_copy(ctxb_ref, ctxb, l_sems.at[3]))
    local.append(pltpu.make_async_copy(cot_ref, cot, l_sems.at[4]))
    local.append(pltpu.make_async_copy(proj_ref, p_all.at[row_block(d)], l_sems.at[5]))
    for copy in local:
        copy.start()

    barrier = pltpu.get_barrier_semaphore()
    for v in range(1, chips):
        pl.semaphore_signal(barrier, inc=1, device_id={"dp": ahead(v) * 2 + core, "seq": s}, device_id_type=MESH)
    pl.semaphore_signal(barrier, inc=1, device_id={"dp": sibling, "seq": s}, device_id_type=MESH)
    for k in range(1, seq_count):
        pl.semaphore_signal(barrier, inc=1, device_id={"dp": d, "seq": seq_ahead(k)}, device_id_type=MESH)

    slot_ids = lax.broadcasted_iota(jnp.int32, (8, slots), 1)
    bias_all[:, slot_block(s)] = jnp.where(slot_ids < count_ref[...], 0.0, -1e30)
    index_col[...] = jnp.broadcast_to(index_ref[...].astype(jnp.float32), (8, slots)).T
    group = math.gcd(slots, 32)

    @pl.loop(0, slots // group)
    def _(j):
        span = pl.ds(pl.multiple_of(j * group, group), group)
        angles = index_col[span, 0:1] * freq_ref[...]
        shift = jnp.concatenate([jnp.sin(angles), jnp.cos(angles)], axis=1)
        with_pos = tok_ref[span, :].astype(jnp.float32) + shift
        pos[span, :] = with_pos
        own_span = pl.ds(pl.multiple_of(s * slots + j * group, group), group)
        x_all[own_span, :] = layer_norm(with_pos).astype(jnp.bfloat16)

    for copy in local[:3]:
        copy.wait()
    pl.semaphore_wait(barrier, chips - 1 + 1 + seq_count - 1)

    sends = []

    def start(copy):
        copy.start()
        sends.append(copy)

    right, left = seq_ahead(1), seq_behind(1)
    rounds = seq_count // 2

    def ring_piece(place, sems, step, origin, piece, target):
        block = place(origin, piece)
        return pltpu.make_async_remote_copy(
            src_ref=block, dst_ref=block, send_sem=sems.at[0, step, piece], recv_sem=sems.at[1, step, piece],
            device_id={"dp": d, "seq": target}, device_id_type=MESH,
        )

    def ring_start(place, r_sems, l_sems):
        for order in range(2):
            if order == 0 or rounds > 1:
                start(ring_piece(place, r_sems, 0, s, order, right))
                start(ring_piece(place, l_sems, 0, s, 1 - order, left))

    def ring_forward(place, r_sems, l_sems):
        for step in range(1, rounds):
            for order in range(2):
                ring_piece(place, r_sems, step - 1, seq_behind(step), order, right).wait_recv()
                if order == 0 or step < rounds - 1:
                    start(ring_piece(place, r_sems, step, seq_behind(step), order, right))
                ring_piece(place, l_sems, step - 1, seq_ahead(step), 1 - order, left).wait_recv()
                if order == 0 or step < rounds - 1:
                    start(ring_piece(place, l_sems, step, seq_ahead(step), 1 - order, left))

    def ring_finish(place, r_sems, l_sems):
        ring_piece(place, r_sems, rounds - 1, seq_behind(rounds), 0, right).wait_recv()
        ring_piece(place, l_sems, rounds - 1, seq_ahead(rounds), 1, left).wait_recv()

    def x_place(origin, piece):
        half_rows = slots // 2
        return x_all.at[pl.ds(pl.multiple_of(origin * slots + piece * half_rows, half_rows), half_rows)]

    def g_place(origin, piece):
        half_rows = rows // 2
        return g_seq.at[origin, pl.ds(piece * half_rows, half_rows)]

    own_w = w_all.at[row_block(d)]
    own_p = p_all.at[row_block(d)]
    for v in range(1, chips):
        start(to_dp(own_w, own_w, w_sems, v - 1, ahead(v) * 2 + core))
    ring_start(x_place, xr_sems, xl_sems)
    start(to_dp(own_w, own_w, w_fsems, 0, sibling))
    for k in range(1, seq_count):
        spot = bias_all.at[:, slot_block(s)]
        start(to_seq(spot, spot, bias_sems, k - 1, seq_ahead(k)))

    for copy in local[3:]:
        copy.wait()
    keep = lax.broadcasted_iota(jnp.int32, (slots, LANES), 0) < bcount_ref[...]
    keep = jnp.where(keep, 1.0, 0.0)[:, 0:1].astype(jnp.bfloat16)
    cot[...] = cot[...] * keep
    step = math.gcd(width, 256)

    @pl.loop(0, width // step)
    def _(j):
        span = pl.ds(pl.multiple_of(j * step, step), step)
        g_part[span, :] = lax.dot_general(
            ctxb[:, span], cot[...], (((0,), (0,)), ((), ())), preferred_element_type=jnp.float32
        ).astype(jnp.bfloat16)

    for v in list(range(1, chips)) + [0]:
        start(to_dp(g_part.at[row_block(ahead(v) * 2 + 1 - core)], g_sib.at[v], gs_sems, v, sibling))

    def chip_sum(v):
        to_dp(g_sib.at[v], g_sib.at[v], gs_sems, v, sibling).wait_recv()
        mine = g_part[row_block(ahead(v) * 2 + core), :].astype(jnp.float32)
        g_chip[v] = (mine + g_sib[v].astype(jnp.float32)).astype(jnp.bfloat16)

    for v in list(range(1, chips)) + [0]:
        chip_sum(v)

    ring_forward(x_place, xr_sems, xl_sems)

    def forward(whole, sems, fsems):
        for v in range(1, chips):
            block = whole.at[row_block(behind(v) * 2 + core)]
            to_dp(block, block, sems, v - 1, sibling).wait_recv()
            start(to_dp(block, block, fsems, v, sibling))

    def from_sibling(whole, fsems):
        for v in range(chips):
            block = whole.at[row_block(behind(v) * 2 + 1 - core)]
            to_dp(block, block, fsems, v, sibling).wait_recv()

    forward(w_all, w_sems, w_fsems)
    for v in range(1, chips):
        start(to_dp(g_chip.at[v], g_recv.at[v - 1], gr_sems, v - 1, ahead(v) * 2 + core))
    for v in range(1, chips):
        start(to_dp(own_p, own_p, p_sems, v - 1, ahead(v) * 2 + core))
    start(to_dp(own_p, own_p, p_fsems, 0, sibling))
    from_sibling(w_all, w_fsems)

    def project(source):
        qkv[source, :] = jnp.dot(
            x_all[source, :], w_all[...], preferred_element_type=jnp.float32
        ).astype(jnp.bfloat16)

    @pl.loop(0, seq_count)
    def _(k):
        order = jnp.where(k < rounds, k, jnp.where(k == seq_count - 1, rounds, k + 1))

        @pl.when(k == seq_count - 1)
        def _():
            ring_finish(x_place, xr_sems, xl_sems)

        project(slot_block(seq_behind(order)))

    for k in range(1, seq_count):
        spot = bias_all.at[:, slot_block(seq_behind(k))]
        to_seq(spot, spot, bias_sems, k - 1, s).wait_recv()

    score_scale = LOG2_E / math.sqrt(head_width)

    def attend(query_rows):
        acc[...] = jnp.zeros_like(acc)
        for head in range(heads_here):
            low = (min(offsets) + head * head_width) // LANES * LANES
            high = round_up(max(offsets) + (head + 1) * head_width, LANES)
            columns = lax.broadcasted_iota(jnp.int32, (1, high - low), 1) + (low - head * head_width) - offset
            own = jnp.where((columns >= 0) & (columns < head_width), 1.0, 0.0)
            query = qkv[query_rows, low:high] * own.astype(jnp.bfloat16)
            scores = lax.dot_general(
                query, qkv[:, part + low:part + high], (((1,), (1,)), ((), ())),
                preferred_element_type=jnp.float32,
            )
            scores = scores * score_scale + bias_all[0:1, :]
            exponent = jnp.exp2(scores - jnp.max(scores, axis=1, keepdims=True))
            total = jnp.sum(exponent, axis=1, keepdims=True)
            mixed = jnp.dot(
                exponent.astype(jnp.bfloat16), qkv[:, 2 * part + low:2 * part + high],
                preferred_element_type=jnp.float32,
            )
            acc[:, low:high] += mixed / total * own

    @pl.loop(0, seq_count)
    def _(i):
        target = seq_ahead(i + 1)
        attend(slot_block(target))

        @pl.when(i < seq_count - 1)
        def _():
            ctx_send[i] = acc[...].astype(jnp.bfloat16)
            to_seq(ctx_send.at[i], ctx_all.at[s], c_sems, i, target).start()

        @pl.when(i == seq_count - 1)
        def _():
            ctx_all[s] = acc[...].astype(jnp.bfloat16)

    total = g_chip[0].astype(jnp.float32)
    for v in range(1, chips):
        to_dp(g_recv.at[v - 1], g_recv.at[v - 1], gr_sems, v - 1, sibling).wait_recv()
        total = total + g_recv[v - 1].astype(jnp.float32)
    g_seq[s] = total.astype(jnp.bfloat16)
    ring_start(g_place, ar_sems, al_sems)

    forward(p_all, p_sems, p_fsems)
    from_sibling(p_all, p_fsems)
    for k in range(1, seq_count):
        spot = ctx_all.at[seq_behind(k)]
        to_seq(ctx_send.at[k - 1], spot, c_sems, k - 1, seq_ahead(k)).wait()
    ring_forward(g_place, ar_sems, al_sems)
    half = math.gcd(width, 256)

    @pl.loop(0, width // half)
    def _(j):
        span = pl.ds(pl.multiple_of(j * half, half), half)
        result = pos[:, span]
        for owner in range(seq_count):
            result = result + jnp.dot(
                ctx_all[owner], p_all[starts[owner]:starts[owner] + part, span],
                preferred_element_type=jnp.float32,
            )
        out_ref[:, span] = result.astype(jnp.bfloat16)

    ring_finish(g_place, ar_sems, al_sems)
    total = g_seq[0].astype(jnp.float32)
    for owner in range(1, seq_count):
        total = total + g_seq[owner].astype(jnp.float32)
    grad_ref[...] = total * (1.0 / math.sqrt(dp_count * seq_count * slots))
    for copy in sends:
        copy.wait_send()


def on_device(tokens, tube_index, counts, qkv_weight, proj_weight, ctx_b, cot_b, b_counts):
    slot_cap = tokens.shape[1]
    model_width = tokens.shape[2]
    seq_count = lax.axis_size("seq")
    dp_count = lax.axis_size("dp")
    heads_here = HEADS // seq_count
    head_width = model_width // HEADS
    head_cols = heads_here * head_width
    part, _ = window(model_width, seq_count, head_cols)
    chips = dp_count // 2
    rows = qkv_weight.shape[0]
    rounds = seq_count // 2
    places = jnp.arange(model_width // 2, dtype=jnp.float32)
    frequency = jnp.exp(places * (-2.0 * math.log(10000.0) / model_width))[None, :]
    in_vmem = pl.BlockSpec(memory_space=pltpu.VMEM)
    in_place = pl.BlockSpec(memory_space=pl.ANY)
    bf16, f32 = jnp.bfloat16, jnp.float32
    out_a, weight_grad = pl.pallas_call(
        functools.partial(block_kernel, dp_count, seq_count, heads_here, head_width),
        out_shape=(
            jax.ShapeDtypeStruct((slot_cap, model_width), bf16),
            jax.ShapeDtypeStruct((rows, model_width), f32),
        ),
        in_specs=[in_vmem] * 5 + [in_place] * 4,
        out_specs=(in_vmem, in_vmem),
        scratch_shapes=[
            pltpu.VMEM((seq_count * slot_cap, model_width), bf16),
            pltpu.VMEM((8, seq_count * slot_cap), f32),
            pltpu.VMEM((model_width, 3 * part), bf16),
            pltpu.VMEM((model_width, model_width), bf16),
            pltpu.VMEM((seq_count * slot_cap, 3 * part), bf16),
            pltpu.VMEM((slot_cap, part), f32),
            pltpu.VMEM((seq_count - 1, slot_cap, part), bf16),
            pltpu.VMEM((seq_count, slot_cap, part), bf16),
            pltpu.VMEM((model_width, model_width), bf16),
            pltpu.VMEM((chips, rows, model_width), bf16),
            pltpu.VMEM((chips, rows, model_width), bf16),
            pltpu.VMEM((chips - 1, rows, model_width), bf16),
            pltpu.VMEM((seq_count, rows, model_width), bf16),
            pltpu.VMEM((slot_cap, model_width), f32),
            pltpu.VMEM((slot_cap, 8), f32),
            pltpu.VMEM((slot_cap, model_width), bf16),
            pltpu.VMEM((slot_cap, model_width), bf16),
            pltpu.SemaphoreType.DMA((6,)),
            pltpu.SemaphoreType.DMA((2, rounds, 2)),
            pltpu.SemaphoreType.DMA((2, rounds, 2)),
            pltpu.SemaphoreType.DMA((2, seq_count - 1)),
            pltpu.SemaphoreType.DMA((2, chips - 1)),
            pltpu.SemaphoreType.DMA((2, chips)),
            pltpu.SemaphoreType.DMA((2, chips - 1)),
            pltpu.SemaphoreType.DMA((2, chips)),
            pltpu.SemaphoreType.DMA((2, seq_count - 1)),
            pltpu.SemaphoreType.DMA((2, chips)),
            pltpu.SemaphoreType.DMA((2, chips - 1)),
            pltpu.SemaphoreType.DMA((2, rounds, 2)),
            pltpu.SemaphoreType.DMA((2, rounds, 2)),
        ],
        compiler_params=pltpu.CompilerParams(
            collective_id=0, has_side_effects=True, vmem_limit_bytes=60 * 1024 * 1024
        ),
        name="attention_block",
    )(tokens[0], tube_index, frequency, counts, b_counts, qkv_weight, proj_weight, ctx_b[0], cot_b[0])
    return (out_a[None], weight_grad)


def solution(mesh):
    in_specs = (
        P("dp", "seq", None),
        P("dp", "seq"),
        P("dp", "seq"),
        P("dp", None),
        P("dp", None),
        P("dp", "seq", None),
        P("dp", "seq", None),
        P("dp", "seq"),
    )
    out_specs = (P("dp", "seq", None), P("dp", None))
    return jax.shard_map(
        on_device, mesh=mesh, in_specs=in_specs, out_specs=out_specs, check_vma=False
    )
```

```python
import functools
import math

import jax
import jax.numpy as jnp
from jax import lax
from jax.experimental import pallas as pl
from jax.experimental.pallas import tpu as pltpu
from jax.sharding import PartitionSpec as P

HEADS = 16


def layer_norm(values):
    centered = values - jnp.mean(values, axis=1, keepdims=True)
    spread = jnp.mean(centered * centered, axis=1, keepdims=True)
    return centered * lax.rsqrt(spread + 1e-06)


LANES = 128
MESH = pl.DeviceIdType.MESH
LOG2_E = math.log2(math.e)


def round_up(value, unit):
    return (value + unit - 1) // unit * unit


def window(width, seq_count, head_cols):
    size = max(owner * head_cols % LANES + head_cols for owner in range(seq_count))
    size = round_up(size, LANES)
    return size, [min(owner * head_cols // LANES * LANES, width - size) for owner in range(seq_count)]


def block_kernel(
    dp_count, seq_count, heads_here, head_width,
    tok_ref, index_ref, freq_ref, count_ref, bcount_ref, w_ref, proj_ref, ctxb_ref, cot_ref,
    out_ref, grad_ref,
    x_all, bias_all, w_all, p_all, qkv, acc, ctx_send, ctx_all,
    g_part, g_sib, g_chip, g_recv, g_seq, g_in, g_out, pos, index_col, ctxb, cot,
    l_sems, xr_sems, xl_sems, bias_sems, w_sems, w_fsems, p_sems, p_fsems, c_sems, gs_sems, gr_sems,
    ar_sems, al_sems,
):
    d = lax.axis_index("dp")
    s = lax.axis_index("seq")
    core = lax.rem(d, 2)
    chip = lax.div(d, 2)
    chips = dp_count // 2
    sibling = chip * 2 + 1 - core
    slots, width = tok_ref.shape
    rows = w_ref.shape[0]
    head_cols = heads_here * head_width
    part, starts = window(width, seq_count, head_cols)
    offsets = [owner * head_cols - start for owner, start in enumerate(starts)]
    first_lane = lax.min(lax.div(s * head_cols, LANES) * LANES, width - part)
    offset = s * head_cols - first_lane

    def ahead(v):
        return lax.rem(chip + v, chips)

    def behind(v):
        return lax.rem(chip + chips - v, chips)

    def seq_ahead(k):
        return lax.rem(s + k, seq_count)

    def seq_behind(k):
        return lax.rem(s + seq_count - k, seq_count)

    def row_block(index):
        return pl.ds(pl.multiple_of(index * rows, rows), rows)

    def slot_block(index):
        return pl.ds(pl.multiple_of(index * slots, slots), slots)

    def to_dp(src, dst, sems, index, target):
        return pltpu.make_async_remote_copy(
            src_ref=src, dst_ref=dst, send_sem=sems.at[0, index], recv_sem=sems.at[1, index],
            device_id={"dp": target, "seq": s}, device_id_type=MESH,
        )

    def to_seq(src, dst, sems, index, target):
        return pltpu.make_async_remote_copy(
            src_ref=src, dst_ref=dst, send_sem=sems.at[0, index], recv_sem=sems.at[1, index],
            device_id={"dp": d, "seq": target}, device_id_type=MESH,
        )

    local = [
        pltpu.make_async_copy(
            w_ref.at[:, pl.ds(pl.multiple_of(kind * width + first_lane, LANES), part)],
            w_all.at[row_block(d), kind * part:(kind + 1) * part], l_sems.at[kind],
        )
        for kind in range(3)
    ]
    local.append(pltpu.make_async_copy(ctxb_ref, ctxb, l_sems.at[3]))
    local.append(pltpu.make_async_copy(cot_ref, cot, l_sems.at[4]))
    local.append(pltpu.make_async_copy(proj_ref, p_all.at[row_block(d)], l_sems.at[5]))
    for copy in local:
        copy.start()

    barrier = pltpu.get_barrier_semaphore()
    for v in range(1, chips):
        pl.semaphore_signal(barrier, inc=1, device_id={"dp": ahead(v) * 2 + core, "seq": s}, device_id_type=MESH)
    pl.semaphore_signal(barrier, inc=1, device_id={"dp": sibling, "seq": s}, device_id_type=MESH)
    for k in range(1, seq_count):
        pl.semaphore_signal(barrier, inc=1, device_id={"dp": d, "seq": seq_ahead(k)}, device_id_type=MESH)

    slot_ids = lax.broadcasted_iota(jnp.int32, (8, slots), 1)
    bias_all[:, slot_block(s)] = jnp.where(slot_ids < count_ref[...], 0.0, -1e30)
    index_col[...] = jnp.broadcast_to(index_ref[...].astype(jnp.float32), (8, slots)).T
    group = math.gcd(slots, 32)

    @pl.loop(0, slots // group)
    def _(j):
        span = pl.ds(pl.multiple_of(j * group, group), group)
        angles = index_col[span, 0:1] * freq_ref[...]
        shift = jnp.concatenate([jnp.sin(angles), jnp.cos(angles)], axis=1)
        with_pos = tok_ref[span, :].astype(jnp.float32) + shift
        pos[span, :] = with_pos
        own_span = pl.ds(pl.multiple_of(s * slots + j * group, group), group)
        x_all[own_span, :] = layer_norm(with_pos).astype(jnp.bfloat16)

    for copy in local[:3]:
        copy.wait()
    pl.semaphore_wait(barrier, chips - 1 + 1 + seq_count - 1)

    sends = []

    def start(copy):
        copy.start()
        sends.append(copy)

    right, left = seq_ahead(1), seq_behind(1)
    rounds = seq_count // 2

    def ring_piece(place, sems, step, origin, piece, target):
        block = place(origin, piece)
        return pltpu.make_async_remote_copy(
            src_ref=block, dst_ref=block, send_sem=sems.at[0, step, piece], recv_sem=sems.at[1, step, piece],
            device_id={"dp": d, "seq": target}, device_id_type=MESH,
        )

    def ring_start(place, r_sems, l_sems):
        for order in range(2):
            if order == 0 or rounds > 1:
                start(ring_piece(place, r_sems, 0, s, order, right))
                start(ring_piece(place, l_sems, 0, s, 1 - order, left))

    def ring_forward(place, r_sems, l_sems):
        for step in range(1, rounds):
            for order in range(2):
                ring_piece(place, r_sems, step - 1, seq_behind(step), order, right).wait_recv()
                if order == 0 or step < rounds - 1:
                    start(ring_piece(place, r_sems, step, seq_behind(step), order, right))
                ring_piece(place, l_sems, step - 1, seq_ahead(step), 1 - order, left).wait_recv()
                if order == 0 or step < rounds - 1:
                    start(ring_piece(place, l_sems, step, seq_ahead(step), 1 - order, left))

    def ring_finish(place, r_sems, l_sems):
        ring_piece(place, r_sems, rounds - 1, seq_behind(rounds), 0, right).wait_recv()
        ring_piece(place, l_sems, rounds - 1, seq_ahead(rounds), 1, left).wait_recv()

    def x_place(origin, piece):
        half_rows = slots // 2
        return x_all.at[pl.ds(pl.multiple_of(origin * slots + piece * half_rows, half_rows), half_rows)]

    own_w = w_all.at[row_block(d)]
    own_p = p_all.at[row_block(d)]
    for v in range(1, chips):
        start(to_dp(own_w, own_w, w_sems, v - 1, ahead(v) * 2 + core))
    ring_start(x_place, xr_sems, xl_sems)
    start(to_dp(own_w, own_w, w_fsems, 0, sibling))
    for k in range(1, seq_count):
        spot = bias_all.at[:, slot_block(s)]
        start(to_seq(spot, spot, bias_sems, k - 1, seq_ahead(k)))

    for copy in local[3:]:
        copy.wait()
    keep = lax.broadcasted_iota(jnp.int32, (slots, LANES), 0) < bcount_ref[...]
    keep = jnp.where(keep, 1.0, 0.0)[:, 0:1].astype(jnp.bfloat16)
    cot[...] = cot[...] * keep
    step = math.gcd(width, 256)

    @pl.loop(0, width // step)
    def _(j):
        span = pl.ds(pl.multiple_of(j * step, step), step)
        g_part[span, :] = lax.dot_general(
            ctxb[:, span], cot[...], (((0,), (0,)), ((), ())), preferred_element_type=jnp.float32
        ).astype(jnp.bfloat16)

    for v in list(range(1, chips)) + [0]:
        start(to_dp(g_part.at[row_block(ahead(v) * 2 + 1 - core)], g_sib.at[v], gs_sems, v, sibling))

    def chip_sum(v):
        to_dp(g_sib.at[v], g_sib.at[v], gs_sems, v, sibling).wait_recv()
        mine = g_part[row_block(ahead(v) * 2 + core), :].astype(jnp.float32)
        g_chip[v] = (mine + g_sib[v].astype(jnp.float32)).astype(jnp.bfloat16)

    for v in list(range(1, chips)) + [0]:
        chip_sum(v)


    def forward(whole, sems, fsems):
        for v in range(1, chips):
            block = whole.at[row_block(behind(v) * 2 + core)]
            to_dp(block, block, sems, v - 1, sibling).wait_recv()
            start(to_dp(block, block, fsems, v, sibling))

    def from_sibling(whole, fsems):
        for v in range(chips):
            block = whole.at[row_block(behind(v) * 2 + 1 - core)]
            to_dp(block, block, fsems, v, sibling).wait_recv()

    forward(w_all, w_sems, w_fsems)
    for v in range(1, chips):
        start(to_dp(g_chip.at[v], g_recv.at[v - 1], gr_sems, v - 1, ahead(v) * 2 + core))
    for v in range(1, chips):
        start(to_dp(own_p, own_p, p_sems, v - 1, ahead(v) * 2 + core))
    start(to_dp(own_p, own_p, p_fsems, 0, sibling))
    ring_forward(x_place, xr_sems, xl_sems)
    from_sibling(w_all, w_fsems)

    def project(source):
        qkv[source, :] = jnp.dot(
            x_all[source, :], w_all[...], preferred_element_type=jnp.float32
        ).astype(jnp.bfloat16)

    @pl.loop(0, seq_count)
    def _(k):
        order = jnp.where(k < rounds, k, jnp.where(k == seq_count - 1, rounds, k + 1))

        @pl.when(k == seq_count - 1)
        def _():
            ring_finish(x_place, xr_sems, xl_sems)

        project(slot_block(seq_behind(order)))

    for k in range(1, seq_count):
        spot = bias_all.at[:, slot_block(seq_behind(k))]
        to_seq(spot, spot, bias_sems, k - 1, s).wait_recv()

    for v in range(1, chips):
        to_dp(g_recv.at[v - 1], g_recv.at[v - 1], gr_sems, v - 1, sibling).wait_recv()
    piece_rows = rows // seq_count
    for owner in range(seq_count):
        span = slice(owner * piece_rows, (owner + 1) * piece_rows)
        total = g_chip[0, span].astype(jnp.float32)
        for v in range(1, chips):
            total = total + g_recv[v - 1, span].astype(jnp.float32)
        g_seq[owner] = total.astype(jnp.bfloat16)
    for k in range(1, seq_count):
        start(to_seq(g_seq.at[seq_ahead(k)], g_in.at[s], ar_sems, k - 1, seq_ahead(k)))

    score_scale = LOG2_E / math.sqrt(head_width)

    def attend(query_rows):
        acc[...] = jnp.zeros_like(acc)
        for head in range(heads_here):
            low = (min(offsets) + head * head_width) // LANES * LANES
            high = round_up(max(offsets) + (head + 1) * head_width, LANES)
            columns = lax.broadcasted_iota(jnp.int32, (1, high - low), 1) + (low - head * head_width) - offset
            own = jnp.where((columns >= 0) & (columns < head_width), 1.0, 0.0)
            query = qkv[query_rows, low:high] * own.astype(jnp.bfloat16)
            scores = lax.dot_general(
                query, qkv[:, part + low:part + high], (((1,), (1,)), ((), ())),
                preferred_element_type=jnp.float32,
            )
            scores = scores * score_scale + bias_all[0:1, :]
            exponent = jnp.exp2(scores - jnp.max(scores, axis=1, keepdims=True))
            total = jnp.sum(exponent, axis=1, keepdims=True)
            mixed = jnp.dot(
                exponent.astype(jnp.bfloat16), qkv[:, 2 * part + low:2 * part + high],
                preferred_element_type=jnp.float32,
            )
            acc[:, low:high] += mixed / total * own

    @pl.loop(0, seq_count)
    def _(i):
        target = seq_ahead(i + 1)
        attend(slot_block(target))

        @pl.when(i < seq_count - 1)
        def _():
            ctx_send[i] = acc[...].astype(jnp.bfloat16)
            to_seq(ctx_send.at[i], ctx_all.at[s], c_sems, i, target).start()

        @pl.when(i == seq_count - 1)
        def _():
            ctx_all[s] = acc[...].astype(jnp.bfloat16)

    for k in range(1, seq_count):
        spot = g_in.at[seq_behind(k)]
        to_seq(spot, spot, ar_sems, k - 1, s).wait_recv()
    g_in[s] = g_seq[s]
    total = g_in[0].astype(jnp.float32)
    for owner in range(1, seq_count):
        total = total + g_in[owner].astype(jnp.float32)
    g_out[s] = total.astype(jnp.bfloat16)
    for k in range(1, seq_count):
        start(to_seq(g_out.at[s], g_out.at[s], al_sems, k - 1, seq_ahead(k)))

    forward(p_all, p_sems, p_fsems)
    from_sibling(p_all, p_fsems)
    for k in range(1, seq_count):
        spot = ctx_all.at[seq_behind(k)]
        to_seq(ctx_send.at[k - 1], spot, c_sems, k - 1, seq_ahead(k)).wait()
    half = math.gcd(width, 256)

    @pl.loop(0, width // half)
    def _(j):
        span = pl.ds(pl.multiple_of(j * half, half), half)
        result = pos[:, span]
        for owner in range(seq_count):
            result = result + jnp.dot(
                ctx_all[owner], p_all[starts[owner]:starts[owner] + part, span],
                preferred_element_type=jnp.float32,
            )
        out_ref[:, span] = result.astype(jnp.bfloat16)

    for k in range(1, seq_count):
        spot = g_out.at[seq_behind(k)]
        to_seq(spot, spot, al_sems, k - 1, s).wait_recv()
    factor = 1.0 / math.sqrt(dp_count * seq_count * slots)
    for owner in range(seq_count):
        grad_ref[owner * piece_rows:(owner + 1) * piece_rows, :] = g_out[owner].astype(jnp.float32) * factor
    for copy in sends:
        copy.wait_send()


def on_device(tokens, tube_index, counts, qkv_weight, proj_weight, ctx_b, cot_b, b_counts):
    slot_cap = tokens.shape[1]
    model_width = tokens.shape[2]
    seq_count = lax.axis_size("seq")
    dp_count = lax.axis_size("dp")
    heads_here = HEADS // seq_count
    head_width = model_width // HEADS
    head_cols = heads_here * head_width
    part, _ = window(model_width, seq_count, head_cols)
    chips = dp_count // 2
    rows = qkv_weight.shape[0]
    rounds = seq_count // 2
    places = jnp.arange(model_width // 2, dtype=jnp.float32)
    frequency = jnp.exp(places * (-2.0 * math.log(10000.0) / model_width))[None, :]
    in_vmem = pl.BlockSpec(memory_space=pltpu.VMEM)
    in_place = pl.BlockSpec(memory_space=pl.ANY)
    bf16, f32 = jnp.bfloat16, jnp.float32
    out_a, weight_grad = pl.pallas_call(
        functools.partial(block_kernel, dp_count, seq_count, heads_here, head_width),
        out_shape=(
            jax.ShapeDtypeStruct((slot_cap, model_width), bf16),
            jax.ShapeDtypeStruct((rows, model_width), f32),
        ),
        in_specs=[in_vmem] * 5 + [in_place] * 4,
        out_specs=(in_vmem, in_vmem),
        scratch_shapes=[
            pltpu.VMEM((seq_count * slot_cap, model_width), bf16),
            pltpu.VMEM((8, seq_count * slot_cap), f32),
            pltpu.VMEM((model_width, 3 * part), bf16),
            pltpu.VMEM((model_width, model_width), bf16),
            pltpu.VMEM((seq_count * slot_cap, 3 * part), bf16),
            pltpu.VMEM((slot_cap, part), f32),
            pltpu.VMEM((seq_count - 1, slot_cap, part), bf16),
            pltpu.VMEM((seq_count, slot_cap, part), bf16),
            pltpu.VMEM((model_width, model_width), bf16),
            pltpu.VMEM((chips, rows, model_width), bf16),
            pltpu.VMEM((chips, rows, model_width), bf16),
            pltpu.VMEM((chips - 1, rows, model_width), bf16),
            pltpu.VMEM((seq_count, rows // seq_count, model_width), bf16),
            pltpu.VMEM((seq_count, rows // seq_count, model_width), bf16),
            pltpu.VMEM((seq_count, rows // seq_count, model_width), bf16),
            pltpu.VMEM((slot_cap, model_width), f32),
            pltpu.VMEM((slot_cap, 8), f32),
            pltpu.VMEM((slot_cap, model_width), bf16),
            pltpu.VMEM((slot_cap, model_width), bf16),
            pltpu.SemaphoreType.DMA((6,)),
            pltpu.SemaphoreType.DMA((2, rounds, 2)),
            pltpu.SemaphoreType.DMA((2, rounds, 2)),
            pltpu.SemaphoreType.DMA((2, seq_count - 1)),
            pltpu.SemaphoreType.DMA((2, chips - 1)),
            pltpu.SemaphoreType.DMA((2, chips)),
            pltpu.SemaphoreType.DMA((2, chips - 1)),
            pltpu.SemaphoreType.DMA((2, chips)),
            pltpu.SemaphoreType.DMA((2, seq_count - 1)),
            pltpu.SemaphoreType.DMA((2, chips)),
            pltpu.SemaphoreType.DMA((2, chips - 1)),
            pltpu.SemaphoreType.DMA((2, seq_count - 1)),
            pltpu.SemaphoreType.DMA((2, seq_count - 1)),
        ],
        compiler_params=pltpu.CompilerParams(
            collective_id=0, has_side_effects=True, vmem_limit_bytes=60 * 1024 * 1024
        ),
        name="attention_block",
    )(tokens[0], tube_index, frequency, counts, b_counts, qkv_weight, proj_weight, ctx_b[0], cot_b[0])
    return (out_a[None], weight_grad)


def solution(mesh):
    in_specs = (
        P("dp", "seq", None),
        P("dp", "seq"),
        P("dp", "seq"),
        P("dp", None),
        P("dp", None),
        P("dp", "seq", None),
        P("dp", "seq", None),
        P("dp", "seq"),
    )
    out_specs = (P("dp", "seq", None), P("dp", None))
    return jax.shard_map(
        on_device, mesh=mesh, in_specs=in_specs, out_specs=out_specs, check_vma=False
    )
```

```python
import functools
import math

import jax
import jax.numpy as jnp
from jax import lax
from jax.experimental import pallas as pl
from jax.experimental.pallas import tpu as pltpu
from jax.sharding import PartitionSpec as P

HEADS = 16


def layer_norm(values):
    centered = values - jnp.mean(values, axis=1, keepdims=True)
    spread = jnp.mean(centered * centered, axis=1, keepdims=True)
    return centered * lax.rsqrt(spread + 1e-06)


LANES = 128
MESH = pl.DeviceIdType.MESH
LOG2_E = math.log2(math.e)


def round_up(value, unit):
    return (value + unit - 1) // unit * unit


def window(width, seq_count, head_cols):
    size = max(owner * head_cols % LANES + head_cols for owner in range(seq_count))
    size = round_up(size, LANES)
    return size, [min(owner * head_cols // LANES * LANES, width - size) for owner in range(seq_count)]


def block_kernel(
    dp_count, seq_count, heads_here, head_width,
    tok_ref, index_ref, freq_ref, count_ref, bcount_ref, w_ref, proj_ref, ctxb_ref, cot_ref,
    out_ref, grad_ref,
    x_all, bias_all, w_all, p_all, qkv, acc, ctx_send, ctx_all,
    g_part, g_sib, g_chip, g_recv, g_seq, g_in, g_out, pos, index_col, ctxb, cot,
    l_sems, xr_sems, xl_sems, bias_sems, w_sems, w_fsems, p_sems, p_fsems, c_sems, gs_sems, gr_sems,
    ar_sems, al_sems, ab_sems, ac_sems,
):
    d = lax.axis_index("dp")
    s = lax.axis_index("seq")
    core = lax.rem(d, 2)
    chip = lax.div(d, 2)
    chips = dp_count // 2
    sibling = chip * 2 + 1 - core
    slots, width = tok_ref.shape
    rows = w_ref.shape[0]
    head_cols = heads_here * head_width
    part, starts = window(width, seq_count, head_cols)
    offsets = [owner * head_cols - start for owner, start in enumerate(starts)]
    first_lane = lax.min(lax.div(s * head_cols, LANES) * LANES, width - part)
    offset = s * head_cols - first_lane

    def ahead(v):
        return lax.rem(chip + v, chips)

    def behind(v):
        return lax.rem(chip + chips - v, chips)

    def seq_ahead(k):
        return lax.rem(s + k, seq_count)

    def seq_behind(k):
        return lax.rem(s + seq_count - k, seq_count)

    def row_block(index):
        return pl.ds(pl.multiple_of(index * rows, rows), rows)

    def slot_block(index):
        return pl.ds(pl.multiple_of(index * slots, slots), slots)

    def to_dp(src, dst, sems, index, target):
        return pltpu.make_async_remote_copy(
            src_ref=src, dst_ref=dst, send_sem=sems.at[0, index], recv_sem=sems.at[1, index],
            device_id={"dp": target, "seq": s}, device_id_type=MESH,
        )

    def to_seq(src, dst, sems, index, target):
        return pltpu.make_async_remote_copy(
            src_ref=src, dst_ref=dst, send_sem=sems.at[0, index], recv_sem=sems.at[1, index],
            device_id={"dp": d, "seq": target}, device_id_type=MESH,
        )

    local = [
        pltpu.make_async_copy(
            w_ref.at[:, pl.ds(pl.multiple_of(kind * width + first_lane, LANES), part)],
            w_all.at[row_block(d), kind * part:(kind + 1) * part], l_sems.at[kind],
        )
        for kind in range(3)
    ]
    local.append(pltpu.make_async_copy(ctxb_ref, ctxb, l_sems.at[3]))
    local.append(pltpu.make_async_copy(cot_ref, cot, l_sems.at[4]))
    local.append(pltpu.make_async_copy(proj_ref, p_all.at[row_block(d)], l_sems.at[5]))
    for copy in local:
        copy.start()

    barrier = pltpu.get_barrier_semaphore()
    for v in range(1, chips):
        pl.semaphore_signal(barrier, inc=1, device_id={"dp": ahead(v) * 2 + core, "seq": s}, device_id_type=MESH)
    pl.semaphore_signal(barrier, inc=1, device_id={"dp": sibling, "seq": s}, device_id_type=MESH)
    for k in range(1, seq_count):
        pl.semaphore_signal(barrier, inc=1, device_id={"dp": d, "seq": seq_ahead(k)}, device_id_type=MESH)

    slot_ids = lax.broadcasted_iota(jnp.int32, (8, slots), 1)
    bias_all[:, slot_block(s)] = jnp.where(slot_ids < count_ref[...], 0.0, -1e30)
    index_col[...] = jnp.broadcast_to(index_ref[...].astype(jnp.float32), (8, slots)).T
    group = math.gcd(slots, 32)

    @pl.loop(0, slots // group)
    def _(j):
        span = pl.ds(pl.multiple_of(j * group, group), group)
        angles = index_col[span, 0:1] * freq_ref[...]
        shift = jnp.concatenate([jnp.sin(angles), jnp.cos(angles)], axis=1)
        with_pos = tok_ref[span, :].astype(jnp.float32) + shift
        pos[span, :] = with_pos
        own_span = pl.ds(pl.multiple_of(s * slots + j * group, group), group)
        x_all[own_span, :] = layer_norm(with_pos).astype(jnp.bfloat16)

    for copy in local[:3]:
        copy.wait()
    pl.semaphore_wait(barrier, chips - 1 + 1 + seq_count - 1)

    sends = []

    def start(copy):
        copy.start()
        sends.append(copy)

    last_hop = seq_count - 2

    def line_copy(side, hop, origin):
        block = x_all.at[slot_block(lax.rem(origin + 2 * seq_count, seq_count))]
        sems = xr_sems if side > 0 else xl_sems
        target = lax.rem(s + side + seq_count, seq_count)
        return to_seq(block, block, sems, hop, target)

    def line_sends(side, hop):
        origin = s - side * hop
        neighbour = s + side
        return (origin >= 0) & (origin < seq_count) & (neighbour >= 0) & (neighbour < seq_count)

    def line_start(hop):
        for side in (1, -1):
            @pl.when(line_sends(side, hop))
            def _():
                line_copy(side, hop, s - side * hop).start()

    def line_arrive(hop):
        for side in (1, -1):
            origin = s - side * (hop + 1)

            @pl.when((origin >= 0) & (origin < seq_count))
            def _():
                line_copy(side, hop, origin).wait_recv()

    def line_pass(hop):
        line_arrive(hop - 1)
        line_start(hop)

    def line_sent():
        for hop in range(last_hop + 1):
            for side in (1, -1):
                @pl.when(line_sends(side, hop))
                def _():
                    line_copy(side, hop, s - side * hop).wait_send()

    own_w = w_all.at[row_block(d)]
    own_p = p_all.at[row_block(d)]
    for v in range(1, chips):
        start(to_dp(own_w, own_w, w_sems, v - 1, ahead(v) * 2 + core))
    line_start(0)
    start(to_dp(own_w, own_w, w_fsems, 0, sibling))
    for k in range(1, seq_count):
        spot = bias_all.at[:, slot_block(s)]
        start(to_seq(spot, spot, bias_sems, k - 1, seq_ahead(k)))

    for copy in local[3:]:
        copy.wait()
    keep = lax.broadcasted_iota(jnp.int32, (slots, LANES), 0) < bcount_ref[...]
    keep = jnp.where(keep, 1.0, 0.0)[:, 0:1].astype(jnp.bfloat16)
    cot[...] = cot[...] * keep
    step = math.gcd(width, 256)

    @pl.loop(0, width // step)
    def _(j):
        span = pl.ds(pl.multiple_of(j * step, step), step)
        g_part[span, :] = lax.dot_general(
            ctxb[:, span], cot[...], (((0,), (0,)), ((), ())), preferred_element_type=jnp.float32
        ).astype(jnp.bfloat16)

    for v in list(range(1, chips)) + [0]:
        start(to_dp(g_part.at[row_block(ahead(v) * 2 + 1 - core)], g_sib.at[v], gs_sems, v, sibling))

    def chip_sum(v):
        to_dp(g_sib.at[v], g_sib.at[v], gs_sems, v, sibling).wait_recv()
        mine = g_part[row_block(ahead(v) * 2 + core), :].astype(jnp.float32)
        g_chip[v] = (mine + g_sib[v].astype(jnp.float32)).astype(jnp.bfloat16)

    for v in list(range(1, chips)) + [0]:
        chip_sum(v)


    def forward(whole, sems, fsems):
        for v in range(1, chips):
            block = whole.at[row_block(behind(v) * 2 + core)]
            to_dp(block, block, sems, v - 1, sibling).wait_recv()
            start(to_dp(block, block, fsems, v, sibling))

    def from_sibling(whole, fsems):
        for v in range(chips):
            block = whole.at[row_block(behind(v) * 2 + 1 - core)]
            to_dp(block, block, fsems, v, sibling).wait_recv()

    if last_hop >= 1:
        line_pass(1)
    forward(w_all, w_sems, w_fsems)
    for v in range(1, chips):
        start(to_dp(g_chip.at[v], g_recv.at[v - 1], gr_sems, v - 1, ahead(v) * 2 + core))
    for v in range(1, chips):
        start(to_dp(own_p, own_p, p_sems, v - 1, ahead(v) * 2 + core))
    start(to_dp(own_p, own_p, p_fsems, 0, sibling))
    from_sibling(w_all, w_fsems)
    for hop in range(2, last_hop + 1):
        line_pass(hop)

    half_rows = rows // 2
    owners = (seq_count // 2 - 1, seq_count // 2)

    def grad_copy(half, sender):
        return pltpu.make_async_remote_copy(
            src_ref=g_seq.at[half], dst_ref=g_in.at[sender], send_sem=ar_sems.at[half], recv_sem=al_sems.at[sender],
            device_id={"dp": d, "seq": owners[half]}, device_id_type=MESH,
        )

    for v in range(1, chips):
        to_dp(g_recv.at[v - 1], g_recv.at[v - 1], gr_sems, v - 1, sibling).wait_recv()
    for half in range(2):
        span = slice(half * half_rows, (half + 1) * half_rows)
        total = g_chip[0, span].astype(jnp.float32)
        for v in range(1, chips):
            total = total + g_recv[v - 1, span].astype(jnp.float32)
        g_seq[half] = total.astype(jnp.bfloat16)

        @pl.when(s != owners[half])
        def _():
            grad_copy(half, s).start()

    def project(source):
        qkv[source, :] = jnp.dot(
            x_all[source, :], w_all[...], preferred_element_type=jnp.float32
        ).astype(jnp.bfloat16)

    @pl.loop(0, seq_count)
    def _(k):
        @pl.when(k == seq_count - 1)
        def _():
            line_arrive(last_hop)

        project(slot_block(jnp.where(s == seq_count - 1, seq_behind(k), seq_ahead(k))))

    for k in range(1, seq_count):
        spot = bias_all.at[:, slot_block(seq_behind(k))]
        to_seq(spot, spot, bias_sems, k - 1, s).wait_recv()

    score_scale = LOG2_E / math.sqrt(head_width)

    def attend(query_rows):
        acc[...] = jnp.zeros_like(acc)
        for head in range(heads_here):
            low = (min(offsets) + head * head_width) // LANES * LANES
            high = round_up(max(offsets) + (head + 1) * head_width, LANES)
            columns = lax.broadcasted_iota(jnp.int32, (1, high - low), 1) + (low - head * head_width) - offset
            own = jnp.where((columns >= 0) & (columns < head_width), 1.0, 0.0)
            query = qkv[query_rows, low:high] * own.astype(jnp.bfloat16)
            scores = lax.dot_general(
                query, qkv[:, part + low:part + high], (((1,), (1,)), ((), ())),
                preferred_element_type=jnp.float32,
            )
            scores = scores * score_scale + bias_all[0:1, :]
            exponent = jnp.exp2(scores - jnp.max(scores, axis=1, keepdims=True))
            total = jnp.sum(exponent, axis=1, keepdims=True)
            mixed = jnp.dot(
                exponent.astype(jnp.bfloat16), qkv[:, 2 * part + low:2 * part + high],
                preferred_element_type=jnp.float32,
            )
            acc[:, low:high] += mixed / total * own

    def at_end(index):
        return (index == 0) | (index == seq_count - 1)

    def ctx_copy(i):
        return to_seq(ctx_send.at[i], ctx_all.at[s], c_sems, i, seq_ahead(i + 1))

    @pl.loop(0, seq_count)
    def _(i):
        target = seq_ahead(i + 1)
        attend(slot_block(target))

        @pl.when(i < seq_count - 1)
        def _():
            ctx_send[i] = acc[...].astype(jnp.bfloat16)

            @pl.when(jnp.logical_not(at_end(target)))
            def _():
                ctx_copy(i).start()

        @pl.when(i == seq_count - 1)
        def _():
            ctx_all[s] = acc[...].astype(jnp.bfloat16)

    for half in range(2):
        @pl.when(s == owners[half])
        def _():
            for k in range(1, seq_count):
                grad_copy(half, seq_behind(k)).wait_recv()
            g_in[s] = g_seq[half]
            total = g_in[0].astype(jnp.float32)
            for sender in range(1, seq_count):
                total = total + g_in[sender].astype(jnp.float32)
            g_out[half] = total.astype(jnp.bfloat16)

    def grad_back(half, k):
        return pltpu.make_async_remote_copy(
            src_ref=g_out.at[half], dst_ref=g_out.at[half], send_sem=ab_sems.at[k - 1],
            recv_sem=ac_sems.at[half], device_id={"dp": d, "seq": seq_ahead(k)}, device_id_type=MESH,
        )

    line_sent()
    for k in range(1, seq_count):
        @pl.when(at_end(seq_ahead(k)))
        def _():
            ctx_copy(k - 1).start()
    for half in range(2):
        @pl.when(s == owners[half])
        def _():
            for k in range(1, seq_count):
                grad_back(half, k).start()

    forward(p_all, p_sems, p_fsems)
    from_sibling(p_all, p_fsems)
    for k in range(1, seq_count):
        spot = ctx_all.at[seq_behind(k)]
        to_seq(ctx_send.at[k - 1], spot, c_sems, k - 1, seq_ahead(k)).wait()
    half = math.gcd(width, 256)

    @pl.loop(0, width // half)
    def _(j):
        span = pl.ds(pl.multiple_of(j * half, half), half)
        result = pos[:, span]
        for owner in range(seq_count):
            result = result + jnp.dot(
                ctx_all[owner], p_all[starts[owner]:starts[owner] + part, span],
                preferred_element_type=jnp.float32,
            )
        out_ref[:, span] = result.astype(jnp.bfloat16)

    for half in range(2):
        @pl.when(s != owners[half])
        def _():
            grad_back(half, 1).wait_recv()
            grad_copy(half, s).wait_send()

        @pl.when(s == owners[half])
        def _():
            for k in range(1, seq_count):
                grad_back(half, k).wait_send()

    factor = 1.0 / math.sqrt(dp_count * seq_count * slots)
    for half in range(2):
        grad_ref[half * half_rows:(half + 1) * half_rows, :] = g_out[half].astype(jnp.float32) * factor
    for copy in sends:
        copy.wait_send()


def on_device(tokens, tube_index, counts, qkv_weight, proj_weight, ctx_b, cot_b, b_counts):
    slot_cap = tokens.shape[1]
    model_width = tokens.shape[2]
    seq_count = lax.axis_size("seq")
    dp_count = lax.axis_size("dp")
    heads_here = HEADS // seq_count
    head_width = model_width // HEADS
    head_cols = heads_here * head_width
    part, _ = window(model_width, seq_count, head_cols)
    chips = dp_count // 2
    rows = qkv_weight.shape[0]
    places = jnp.arange(model_width // 2, dtype=jnp.float32)
    frequency = jnp.exp(places * (-2.0 * math.log(10000.0) / model_width))[None, :]
    in_vmem = pl.BlockSpec(memory_space=pltpu.VMEM)
    in_place = pl.BlockSpec(memory_space=pl.ANY)
    bf16, f32 = jnp.bfloat16, jnp.float32
    out_a, weight_grad = pl.pallas_call(
        functools.partial(block_kernel, dp_count, seq_count, heads_here, head_width),
        out_shape=(
            jax.ShapeDtypeStruct((slot_cap, model_width), bf16),
            jax.ShapeDtypeStruct((rows, model_width), f32),
        ),
        in_specs=[in_vmem] * 5 + [in_place] * 4,
        out_specs=(in_vmem, in_vmem),
        scratch_shapes=[
            pltpu.VMEM((seq_count * slot_cap, model_width), bf16),
            pltpu.VMEM((8, seq_count * slot_cap), f32),
            pltpu.VMEM((model_width, 3 * part), bf16),
            pltpu.VMEM((model_width, model_width), bf16),
            pltpu.VMEM((seq_count * slot_cap, 3 * part), bf16),
            pltpu.VMEM((slot_cap, part), f32),
            pltpu.VMEM((seq_count - 1, slot_cap, part), bf16),
            pltpu.VMEM((seq_count, slot_cap, part), bf16),
            pltpu.VMEM((model_width, model_width), bf16),
            pltpu.VMEM((chips, rows, model_width), bf16),
            pltpu.VMEM((chips, rows, model_width), bf16),
            pltpu.VMEM((chips - 1, rows, model_width), bf16),
            pltpu.VMEM((2, rows // 2, model_width), bf16),
            pltpu.VMEM((seq_count, rows // 2, model_width), bf16),
            pltpu.VMEM((2, rows // 2, model_width), bf16),
            pltpu.VMEM((slot_cap, model_width), f32),
            pltpu.VMEM((slot_cap, 8), f32),
            pltpu.VMEM((slot_cap, model_width), bf16),
            pltpu.VMEM((slot_cap, model_width), bf16),
            pltpu.SemaphoreType.DMA((6,)),
            pltpu.SemaphoreType.DMA((2, seq_count - 1)),
            pltpu.SemaphoreType.DMA((2, seq_count - 1)),
            pltpu.SemaphoreType.DMA((2, seq_count - 1)),
            pltpu.SemaphoreType.DMA((2, chips - 1)),
            pltpu.SemaphoreType.DMA((2, chips)),
            pltpu.SemaphoreType.DMA((2, chips - 1)),
            pltpu.SemaphoreType.DMA((2, chips)),
            pltpu.SemaphoreType.DMA((2, seq_count - 1)),
            pltpu.SemaphoreType.DMA((2, chips)),
            pltpu.SemaphoreType.DMA((2, chips - 1)),
            pltpu.SemaphoreType.DMA((2,)),
            pltpu.SemaphoreType.DMA((seq_count,)),
            pltpu.SemaphoreType.DMA((seq_count - 1,)),
            pltpu.SemaphoreType.DMA((2,)),
        ],
        compiler_params=pltpu.CompilerParams(
            collective_id=0, has_side_effects=True, vmem_limit_bytes=60 * 1024 * 1024
        ),
        name="attention_block",
    )(tokens[0], tube_index, frequency, counts, b_counts, qkv_weight, proj_weight, ctx_b[0], cot_b[0])
    return (out_a[None], weight_grad)


def solution(mesh):
    in_specs = (
        P("dp", "seq", None),
        P("dp", "seq"),
        P("dp", "seq"),
        P("dp", None),
        P("dp", None),
        P("dp", "seq", None),
        P("dp", "seq", None),
        P("dp", "seq"),
    )
    out_specs = (P("dp", "seq", None), P("dp", None))
    return jax.shard_map(
        on_device, mesh=mesh, in_specs=in_specs, out_specs=out_specs, check_vma=False
    )
```
